256 devices in a mesh: rows: 16 (over y, x), mus: 16 (over z, core).
Axes of the slice: x: 4, y: 4, z: 8, core: 2. Of those that a mesh axis runs over, the one named last changes fastest.
Arguments:
- sketch_seed: int32 [1], replicated, may hold values from 0 to 46336
- angles: int32 [6, 12288], P(None, 'rows'), may hold values from 0 to 63
- lengths: float32 [304, 12288], P(None, 'rows'), may hold values from -6 to 6
Outputs:
- coefficients: float32 [304, 462], P('mus')
- residual: float32 [304, 12288], P('mus', 'rows')
The draws below stay inside these ranges and needn't reach their ends.
All inputs are finite; a program needn't handle non-finite values.
Results may differ from the reference program's by a relative error of at most 0.0003.
Values sent between devices are 32-bit elements; how exact they have to be, the bound alone decides.
No kernel may reach another device: no remote copies, remote signals or barrier semaphores. Data moves between devices by JAX's collectives and lax.ppermute only.
A program may use at most 64 MiB of HBM per device.

```python
import math
import jax
import jax.numpy as jnp
from jax import lax

ANGLES = 6
DEGREE = 5
TERMS = 462
MUSCLES = 304
SKETCH = 2048
GRID = 64
ITERS = 3
POSES = 12288


def plant(array, rng, smallest, largest):
    place = [jax.random.randint(jax.random.fold_in(rng, axis), (), 0, length) for axis, length in enumerate(array.shape)]
    widest = array.shape.index(max(array.shape))
    beside = place[:widest] + [(place[widest] + 1) % array.shape[widest]] + place[widest + 1:]
    return array.at[tuple(place)].set(smallest).at[tuple(beside)].set(largest)


def block_scale(own_key, extent, cuts, smallest, largest):
    def one(dim, blocks):
        draws = jax.random.uniform(jax.random.fold_in(jax.random.fold_in(own_key, 6), dim), (blocks,), jnp.float32, smallest / len(cuts), largest / len(cuts))
        return jnp.repeat(jnp.exp(draws), extent[dim] // blocks).reshape((-1,) + (1,) * (len(extent) - dim - 1))

    factor_of = one(*cuts[0])
    for cut in cuts[1:]:
        factor_of = factor_of * one(*cut)
    return factor_of


def centred(key, dims, spread, most, cuts=(), kind=jnp.bfloat16):
    values = jax.random.normal(key, dims, jnp.float32) * spread
    if len(cuts) > 0:
        values = block_scale(key, dims, cuts, -0.22, 0.18) * values
    return jnp.clip(values, min=-most, max=most).astype(kind)


def setup_inputs(seed: int = 0) -> dict:
    key_of = jax.random.split(jax.random.key(seed), 4)
    return {
        "sketch_seed": jax.random.randint(key_of[0], (1,), 0, 46337).astype(jnp.int32),
        "angles": plant(jax.random.randint(key_of[1], (ANGLES, POSES), 0, GRID), jax.random.fold_in(key_of[1], 1), 0, GRID - 1).astype(jnp.int32),
        "lengths": centred(key_of[2], (MUSCLES, POSES), 1.0, 6.0, ((1, 16),), jnp.float32),
    }


modulus = 46337
epsilon = 1e-06

def mix_round(values):
    return (values * values + 7919) % modulus

def sketch_block(seed_value, row_ids, pose_ids):
    row_code = mix_round((row_ids * 389 + seed_value) % modulus)
    pose_code = (pose_ids % modulus * 13 + seed_value) % modulus
    hashed = mix_round(mix_round((row_code[:, None] * 3 + pose_code[None, :]) % modulus))
    return ((hashed.astype(jnp.float32) + 0.5) * (2.0 / modulus) - 1.0) * math.sqrt(3.0 / SKETCH)

def exponent_table():
    tuples = [[]]
    for angle in range(ANGLES):
        tuples = [prefix + [order] for prefix in tuples for order in range(DEGREE + 1) if sum(prefix) + order <= DEGREE]
    return [[entry[angle] for entry in tuples] for angle in range(ANGLES)]

def legendre_basis(indices):
    position = (2.0 * indices.astype(jnp.float32) + 1.0) / GRID - 1.0
    polynomials = [jnp.ones_like(position), position]
    for order in range(1, DEGREE):
        polynomials.append(((2 * order + 1) * position * polynomials[order] - order * polynomials[order - 1]) / (order + 1))
    exponents = exponent_table()
    degrees = jnp.arange(DEGREE + 1, dtype=jnp.int32)
    product = None
    for angle in range(ANGLES):
        legendre = jnp.stack([math.sqrt(2 * order + 1) * polynomials[order][angle] for order in range(DEGREE + 1)])
        selector = (jnp.asarray(exponents[angle], dtype=jnp.int32)[:, None] == degrees[None, :]).astype(jnp.float32)
        factor = jnp.dot(selector, legendre, precision=lax.Precision.HIGHEST)
        product = factor if product is None else product * factor
    return product

def contract_last(left, right):
    return lax.dot_general(left, right, (((1,), (1,)), ((), ())), precision=lax.Precision.HIGHEST)

def contract_first(left, right):
    return lax.dot_general(left, right, (((0,), (0,)), ((), ())), precision=lax.Precision.HIGHEST)

def front_solve(factor_low, values):
    return jax.scipy.linalg.solve_triangular(factor_low, values, lower=True)

def back_solve(factor_low, values):
    return jax.scipy.linalg.solve_triangular(factor_low, values, lower=True, trans=1)

def reference(sketch_seed, angles, lengths):
    basis_scale = 1.0 / math.sqrt(POSES)
    basis = legendre_basis(angles) * basis_scale
    seed_value = sketch_seed[0]
    ref_width = math.gcd(POSES, 2048)
    sketch_ids = jnp.arange(SKETCH, dtype=jnp.int32)

    def sketch_step(block_index, sums):
        offset = block_index.astype(jnp.int32) * ref_width
        basis_block = lax.dynamic_slice_in_dim(basis, offset, ref_width, 1)
        pose_ids = offset + jnp.arange(ref_width, dtype=jnp.int32)
        weights = sketch_block(seed_value, sketch_ids, pose_ids)
        length_block = lax.dynamic_slice_in_dim(lengths, offset, ref_width, 1)
        return (sums[0] + contract_last(weights, basis_block), sums[1] + contract_last(weights, length_block))
    initial = (jnp.zeros((SKETCH, TERMS), jnp.float32), jnp.zeros((SKETCH, MUSCLES), jnp.float32))
    sketched_basis, sketched_lengths = lax.fori_loop(0, POSES // ref_width, sketch_step, initial)
    gram_matrix = contract_first(sketched_basis, sketched_basis)
    factor_low = jnp.linalg.cholesky(gram_matrix)
    start_coef = back_solve(factor_low, front_solve(factor_low, contract_first(sketched_basis, sketched_lengths)))

    def advance(weight, previous, direction):
        fresh_rows = weight[:, None] * previous + contract_first(direction, basis)
        u_norm = jnp.sqrt(lax.optimization_barrier(jnp.sum(fresh_rows * fresh_rows, axis=1)) + epsilon)
        unit_rows = fresh_rows / u_norm[:, None]
        return (unit_rows, u_norm, contract_last(basis, unit_rows))
    unit_rows, u_norm, summed = advance(jnp.ones((MUSCLES,), jnp.float32), lengths, -start_coef)
    q_terms = front_solve(factor_low, summed)
    v_norm = jnp.sqrt(lax.optimization_barrier(jnp.sum(q_terms * q_terms, axis=0)) + epsilon)
    v_terms = q_terms / v_norm[None, :]
    w_terms = v_terms
    phi_bar = u_norm
    rot_bar = v_norm
    y_terms = jnp.zeros((TERMS, MUSCLES), jnp.float32)
    for step_index in range(ITERS):
        unit_rows, u_norm, summed = advance(-v_norm, unit_rows, back_solve(factor_low, v_terms))
        q_terms = front_solve(factor_low, summed) - u_norm[None, :] * v_terms
        v_norm = jnp.sqrt(lax.optimization_barrier(jnp.sum(q_terms * q_terms, axis=0)) + epsilon)
        v_terms = q_terms / v_norm[None, :]
        rot_norm = jnp.sqrt(rot_bar * rot_bar + u_norm * u_norm)
        cosine = rot_bar / rot_norm
        sine_term = u_norm / rot_norm
        rot_theta = sine_term * v_norm
        rot_bar = -cosine * v_norm
        phi_now = cosine * phi_bar
        phi_bar = sine_term * phi_bar
        y_terms = y_terms + (phi_now / rot_norm)[None, :] * w_terms
        w_terms = v_terms - (rot_theta / rot_norm)[None, :] * w_terms
    coef_terms = start_coef + back_solve(factor_low, y_terms)
    residual_rows = lengths - contract_first(coef_terms, basis)
    return (coef_terms.T, residual_rows)
```

```python
import functools
import math

import jax
import jax.numpy as jnp
import numpy as np
from jax import lax
from jax.experimental import pallas as pl
from jax.experimental.pallas import tpu as pltpu
from jax.sharding import PartitionSpec as P

ANGLES = 6
DEGREE = 5
TERMS = 462
MUSCLES = 304
SKETCH = 2048
GRID = 64
ITERS = 3
POSES = 12288

ROWS = 16
MUS = 16
POSE_DEV = POSES // ROWS
OWN = MUSCLES // MUS
SKETCH_DEV = SKETCH // MUS
PAD = 512
FIRST = 464
STACK = FIRST + MUSCLES
BLOCK = PAD // ROWS
PAIR = 32

modulus = 46337
epsilon = 1e-06

f32, bf16, i32 = jnp.float32, jnp.bfloat16, jnp.int32
HIGHEST = lax.Precision.HIGHEST
NN = (((1,), (0,)), ((), ()))
NT = (((1,), (1,)), ((), ()))
TN = (((0,), (0,)), ((), ()))


def exponent_table():
    tuples = [[]]
    for angle in range(ANGLES):
        tuples = [
            prefix + [order]
            for prefix in tuples
            for order in range(DEGREE + 1)
            if sum(prefix) + order <= DEGREE
        ]
    return tuples


PAIRS = [(i, j) for i in range(DEGREE + 1) for j in range(DEGREE + 1 - i)]


def pair_selectors():
    table = np.zeros((3, PAD, 3 * PAIR), np.float32)
    for j, entry in enumerate(exponent_table()):
        for g in range(3):
            at = PAIRS.index((entry[2 * g], entry[2 * g + 1]))
            for piece in range(3):
                table[g, j, piece * PAIR + at] = 1.0
    return table


def split2(x):
    high = x.astype(bf16)
    return high, (x - high.astype(f32)).astype(bf16)


def dot3(a, b, dims):
    (ah, al), (bh, bl) = a, b
    one = functools.partial(lax.dot_general, dimension_numbers=dims, preferred_element_type=f32)
    return one(ah, bh) + (one(ah, bl) + one(al, bh))


def exact(a, b, dims):
    return lax.dot_general(a, b, dims, precision=HIGHEST, preferred_element_type=f32)


def mod_m(x):
    quotient = (x.astype(f32) * (1.0 / modulus) - 0.01).astype(i32)
    rest = x - quotient * modulus
    return jnp.where(rest >= modulus, rest - modulus, rest)


def mix_round(x):
    return mod_m(x * x + 7919)


def local_kernel(sc_ref, ang_ref, len_ref, sel_ref, z_ref, basis_ref, own_ref, pair_ref, stack_ref, right_ref):
    row_rank, mus_rank, seed = sc_ref[0], sc_ref[1], sc_ref[2]
    position = (2.0 * ang_ref[...].astype(f32) + 1.0) / GRID - 1.0
    plain = [jnp.ones_like(position), position]
    for order in range(1, DEGREE):
        plain.append(
            ((2 * order + 1) * position * plain[order] - order * plain[order - 1])
            * (1.0 / (order + 1))
        )
    scaled = [math.sqrt(2 * order + 1) * plain[order] for order in range(DEGREE + 1)]
    pair_ref[...] = jnp.zeros_like(pair_ref)
    for g in range(3):
        for at, (i, j) in enumerate(PAIRS):
            pair_ref[g, at : at + 1, :] = (
                scaled[i][2 * g : 2 * g + 1] * scaled[j][2 * g + 1 : 2 * g + 2]
            )
    product = None
    for g in range(3):
        whole = pair_ref[g]
        high = whole.astype(bf16)
        rest = whole - high.astype(f32)
        mid = rest.astype(bf16)
        low = (rest - mid.astype(f32)).astype(bf16)
        pieces = jnp.concatenate([high, mid, low], axis=0)
        factor = lax.dot_general(sel_ref[g], pieces, NN, preferred_element_type=f32)
        product = factor if product is None else product * factor
    basis = product * (1.0 / math.sqrt(POSES))
    basis_ref[...] = basis
    stack_ref[0:FIRST, :] = basis[0:FIRST]
    stack_ref[FIRST:STACK, :] = len_ref[...]

    sketch_ids = mus_rank * SKETCH_DEV + lax.broadcasted_iota(i32, (SKETCH_DEV, 1), 0)
    pose_ids = row_rank * POSE_DEV + lax.broadcasted_iota(i32, (1, POSE_DEV), 1)
    row_code = mod_m(3 * mix_round(mod_m(sketch_ids * 389 + seed)))
    pose_code = mod_m(mod_m(pose_ids) * 13 + seed)
    code = row_code + pose_code
    code = jnp.where(code >= modulus, code - modulus, code)
    hashed = mix_round(mix_round(code))
    sketch = ((hashed.astype(f32) + 0.5) * (2.0 / modulus) - 1.0) * math.sqrt(3.0 / SKETCH)
    both = dot3(split2(sketch), split2(stack_ref[...]), NT)
    for r in range(ROWS):
        z_ref[r, :, 0:STACK] = both[8 * r : 8 * r + 8]

    own_ref[...] = jnp.zeros_like(own_ref)
    for k in range(OWN):
        own_ref[k : k + 1, :] = len_ref[pl.ds(mus_rank * OWN + k, 1), :]
    right_ref[0:BLOCK, :] = basis_ref[pl.ds(pl.multiple_of(mus_rank * BLOCK, BLOCK), BLOCK), :]
    right_ref[BLOCK : 2 * BLOCK, :] = own_ref[...]
    columns = dot3(split2(basis), split2(right_ref[...]), NT)
    own = own_ref[...]
    squares = exact(jnp.ones((8, POSE_DEV), f32), own * own, NT)
    for r in range(ROWS):
        for k in range(4):
            at = BLOCK * r + 8 * k
            z_ref[r, :, STACK + 64 * k : STACK + 64 * k + 64] = columns[at : at + 8]
    z_ref[ROWS - 1, :, STACK + 192 + BLOCK : STACK + 256] = squares


def gram_kernel(sc_ref, all_ref, out_ref, full_ref, place_ref):
    row_rank, mus_rank = sc_ref[0], sc_ref[1]
    both = jnp.concatenate([all_ref[r, :, 0:STACK] for r in range(ROWS)], axis=0)
    parts = split2(both)
    full_ref[...] = dot3((parts[0][:, 0:PAD], parts[1][:, 0:PAD]), parts, TN)
    out_ref[:, 0:STACK] = full_ref[pl.ds(pl.multiple_of(row_rank * BLOCK, BLOCK), BLOCK), :]
    place_ref[...] = jnp.zeros_like(place_ref)
    for k in range(4):
        place_ref[8 * k : 8 * k + 8, 0:BLOCK] = all_ref[
            row_rank, :, STACK + 64 * k : STACK + 64 * k + BLOCK
        ]
    out_ref[:, STACK : STACK + PAD] = pltpu.roll(place_ref[...], mus_rank * BLOCK, 1)


def solve_kernel(
    sc_ref, mine_ref, theirs_ref, all_ref, basis_ref, own_ref, coef_ref, res_ref,
    whole_ref, m_ref, x_ref, e_ref, c_ref,
):
    mus_rank = sc_ref[1]
    core = lax.rem(mus_rank, 2)
    half = BLOCK // 2

    def assemble(top_ref, bottom_ref):
        for r in range(ROWS):
            whole_ref[BLOCK * r : BLOCK * r + half, :] = top_ref[r]
            whole_ref[BLOCK * r + half : BLOCK * r + BLOCK, :] = bottom_ref[r]

    @pl.when(core == 0)
    def _():
        assemble(mine_ref, theirs_ref)

    @pl.when(core == 1)
    def _():
        assemble(theirs_ref, mine_ref)

    rows = lax.broadcasted_iota(i32, (PAD, PAD), 0)
    cols = lax.broadcasted_iota(i32, (PAD, PAD), 1)
    unit = (rows == cols).astype(f32)
    inside = (rows < TERMS) & (cols < TERMS)
    m_ref[...] = jnp.where(inside, whole_ref[:, 0:PAD], unit)
    c_ref[...] = jnp.zeros_like(c_ref)
    for r in range(ROWS):
        for k in range(4):
            at = BLOCK * r + 8 * k
            c_ref[at : at + 8, 0:BLOCK] = all_ref[
                r, :, STACK + 64 * k + BLOCK : STACK + 64 * k + 64
            ]
    c_all = c_ref[...]
    lengths2 = c_all[PAD - 1 : PAD, :]
    valid = lax.broadcasted_iota(i32, (PAD, 128), 0) < TERMS
    c_own = jnp.where(valid, c_all, 0.0)
    pick = (
        lax.broadcasted_iota(i32, (STACK - 384, 128), 0) + 384
        == lax.broadcasted_iota(i32, (STACK - 384, 128), 1) + FIRST + mus_rank * OWN
    ) & (lax.broadcasted_iota(i32, (STACK - 384, 128), 1) < OWN)
    projected = exact(whole_ref[:, 384:STACK], pick.astype(f32), NN)
    projected = jnp.where(valid, projected, 0.0)

    def plain(a, b):
        return lax.dot_general(a.astype(bf16), b.astype(bf16), NN, preferred_element_type=f32)

    gram = m_ref[...]
    frob = 1.0 / jnp.sqrt(jnp.sum(gram * gram))
    normed = gram * frob
    square = plain(normed, normed)
    fourth = plain(square, square)
    bound = jnp.sqrt(jnp.sqrt(jnp.sqrt(jnp.sum(fourth * fourth))))
    x_ref[...] = unit * (1.84 * frob / bound)

    def coarse(_, carry):
        x = x_ref[...]
        e = unit - plain(m_ref[...], x)
        x_ref[...] = x + plain(x, e)
        return carry

    lax.fori_loop(0, 5, coarse, 0)

    def fine(state):
        step, _ = state
        x = x_ref[...]
        e = unit - exact(m_ref[...], x, NN)
        x_ref[...] = x + plain(x, e)
        return step + 1, jnp.sum(e * e)

    lax.while_loop(lambda s: (s[0] < 40) & (s[1] > 1e-6), fine, (0, jnp.float32(1.0)))

    inv = functools.partial(lambda b: exact(x_ref[...], b, NN))
    e_ref[...] = jnp.where(inside, whole_ref[:, STACK : STACK + PAD], 0.0)
    apply_g = functools.partial(lambda b: exact(e_ref[...], b, NN))

    def total(a):
        return jnp.sum(a, axis=0, keepdims=True)

    start = inv(projected)
    g_start = apply_g(start)
    g_hat = c_own - g_start
    fresh2 = jnp.maximum(lengths2 - total(start * (c_own + g_hat)), 0.0)
    u_norm = jnp.sqrt(fresh2 + epsilon)
    g_hat = g_hat / u_norm
    u_square = fresh2 / (fresh2 + epsilon)
    t = inv(g_hat)
    v_norm = jnp.sqrt(jnp.maximum(total(g_hat * t), 0.0) + epsilon)
    v_hat = g_hat / v_norm
    t = t / v_norm
    w = t
    phi_bar = u_norm
    rot_bar = v_norm
    y = jnp.zeros_like(t)
    for step in range(ITERS):
        g_t = apply_g(t)
        fresh2 = jnp.maximum(
            total(t * (g_t - 2.0 * v_norm * g_hat)) + v_norm * v_norm * u_square, 0.0
        )
        u_norm = jnp.sqrt(fresh2 + epsilon)
        rot_norm = jnp.sqrt(rot_bar * rot_bar + u_norm * u_norm)
        cosine = rot_bar / rot_norm
        sine = u_norm / rot_norm
        y = y + (cosine * phi_bar / rot_norm) * w
        if step == ITERS - 1:
            break
        g_hat = (g_t - v_norm * g_hat) / u_norm
        u_square = fresh2 / (fresh2 + epsilon)
        q_hat = g_hat - u_norm * v_hat
        t = inv(q_hat)
        v_norm = jnp.sqrt(jnp.maximum(total(q_hat * t), 0.0) + epsilon)
        v_hat = q_hat / v_norm
        t = t / v_norm
        w = t - (sine * v_norm / rot_norm) * w
        rot_bar = -cosine * v_norm
        phi_bar = sine * phi_bar
    coef = jnp.transpose(start + y)
    coef_ref[...] = coef[0:OWN, 0:TERMS]
    fitted = exact(coef[0:BLOCK], basis_ref[...], NN)
    res_ref[...] = own_ref[0:OWN, :] - fitted[0:OWN]


def vmem():
    return pl.BlockSpec(memory_space=pltpu.VMEM)


def smem():
    return pl.BlockSpec(memory_space=pltpu.SMEM)


def per_device(sketch_seed, angles, lengths):
    row_rank = lax.axis_index("rows")
    mus_rank = lax.axis_index("mus")
    ranks = jnp.stack([row_rank, mus_rank, sketch_seed[0]]).astype(i32)
    selectors = jnp.asarray(pair_selectors(), dtype=bf16)

    z, basis, own = pl.pallas_call(
        local_kernel,
        out_shape=(
            jax.ShapeDtypeStruct((ROWS, 8, STACK + 256), f32),
            jax.ShapeDtypeStruct((PAD, POSE_DEV), f32),
            jax.ShapeDtypeStruct((BLOCK, POSE_DEV), f32),
        ),
        in_specs=[smem(), vmem(), vmem(), vmem()],
        out_specs=(vmem(), vmem(), vmem()),
        scratch_shapes=[
            pltpu.VMEM((3, PAIR, POSE_DEV), f32),
            pltpu.VMEM((STACK, POSE_DEV), f32),
            pltpu.VMEM((2 * BLOCK, POSE_DEV), f32),
        ],
        name="local_products",
    )(ranks, angles, lengths, selectors)

    summed = jnp.sum(lax.all_to_all(z, "rows", 0, 0), axis=0)
    everyone = lax.all_to_all(
        jnp.broadcast_to(summed[None], (ROWS,) + summed.shape), "rows", 0, 0
    )

    block = pl.pallas_call(
        gram_kernel,
        out_shape=jax.ShapeDtypeStruct((BLOCK, STACK + PAD), f32),
        in_specs=[smem(), vmem()],
        out_specs=vmem(),
        scratch_shapes=[pltpu.VMEM((PAD, STACK), f32), pltpu.VMEM((BLOCK, PAD), f32)],
        name="gram_block",
    )(ranks, everyone)

    for bit in (1, 2, 4, 8):
        block = block + lax.ppermute(block, "mus", [(i, i ^ bit) for i in range(MUS)])

    half = BLOCK // 2
    kept = jnp.where(lax.rem(mus_rank, 2) == 0, block[:half], block[half:])
    mine = lax.all_to_all(jnp.broadcast_to(kept[None], (ROWS,) + kept.shape), "rows", 0, 0)
    theirs = lax.ppermute(mine, "mus", [(i, i ^ 1) for i in range(MUS)])

    coef, residual = pl.pallas_call(
        solve_kernel,
        out_shape=(
            jax.ShapeDtypeStruct((OWN, TERMS), f32),
            jax.ShapeDtypeStruct((OWN, POSE_DEV), f32),
        ),
        in_specs=[smem()] + [vmem()] * 5,
        out_specs=(vmem(), vmem()),
        scratch_shapes=[
            pltpu.VMEM((PAD, STACK + PAD), f32),
            pltpu.VMEM((PAD, PAD), f32),
            pltpu.VMEM((PAD, PAD), f32),
            pltpu.VMEM((PAD, PAD), f32),
            pltpu.VMEM((PAD, 128), f32),
        ],
        name="solve",
    )(ranks, mine, theirs, everyone, basis, own)
    return coef, residual


def solution(mesh):
    placed = (P(), P(None, "rows"), P(None, "rows"))
    return jax.shard_map(
        per_device,
        mesh=mesh,
        in_specs=placed,
        out_specs=(P("mus", None), P("mus", "rows")),
        check_vma=False,
    )
```

```python
import functools
import math

import jax
import jax.numpy as jnp
import numpy as np
from jax import lax
from jax.experimental import pallas as pl
from jax.experimental.pallas import tpu as pltpu
from jax.sharding import PartitionSpec as P

ANGLES = 6
DEGREE = 5
TERMS = 462
MUSCLES = 304
SKETCH = 2048
GRID = 64
ITERS = 3
POSES = 12288

ROWS = 16
MUS = 16
POSE_DEV = POSES // ROWS
OWN = MUSCLES // MUS
SKETCH_DEV = SKETCH // MUS
PAD = 512
FIRST = 464
STACK = FIRST + MUSCLES
BLOCK = PAD // ROWS
PAIR = 32

modulus = 46337
epsilon = 1e-06

f32, bf16, i32 = jnp.float32, jnp.bfloat16, jnp.int32
HIGHEST = lax.Precision.HIGHEST
NN = (((1,), (0,)), ((), ()))
NT = (((1,), (1,)), ((), ()))
TN = (((0,), (0,)), ((), ()))


def exponent_table():
    tuples = [[]]
    for angle in range(ANGLES):
        tuples = [
            prefix + [order]
            for prefix in tuples
            for order in range(DEGREE + 1)
            if sum(prefix) + order <= DEGREE
        ]
    return tuples


PAIRS = [(i, j) for i in range(DEGREE + 1) for j in range(DEGREE + 1 - i)]


def pair_selectors():
    table = np.zeros((3, PAD, 3 * PAIR), np.float32)
    for j, entry in enumerate(exponent_table()):
        for g in range(3):
            at = PAIRS.index((entry[2 * g], entry[2 * g + 1]))
            for piece in range(3):
                table[g, j, piece * PAIR + at] = 1.0
    return table


def split2(x):
    high = x.astype(bf16)
    return high, (x - high.astype(f32)).astype(bf16)


def dot3(a, b, dims):
    (ah, al), (bh, bl) = a, b
    one = functools.partial(lax.dot_general, dimension_numbers=dims, preferred_element_type=f32)
    return one(ah, bh) + (one(ah, bl) + one(al, bh))


def exact(a, b, dims):
    return lax.dot_general(a, b, dims, precision=HIGHEST, preferred_element_type=f32)


def mod_m(x):
    quotient = (x.astype(f32) * (1.0 / modulus) - 0.01).astype(i32)
    rest = x - quotient * modulus
    return jnp.where(rest >= modulus, rest - modulus, rest)


def mix_round(x):
    return mod_m(x * x + 7919)


def local_kernel(sc_ref, ang_ref, len_ref, sel_ref, z_ref, basis_ref, own_ref, pair_ref, stack_ref, right_ref):
    row_rank, mus_rank, seed = sc_ref[0], sc_ref[1], sc_ref[2]
    position = (2.0 * ang_ref[...].astype(f32) + 1.0) / GRID - 1.0
    plain = [jnp.ones_like(position), position]
    for order in range(1, DEGREE):
        plain.append(
            ((2 * order + 1) * position * plain[order] - order * plain[order - 1])
            * (1.0 / (order + 1))
        )
    scaled = [math.sqrt(2 * order + 1) * plain[order] for order in range(DEGREE + 1)]
    pair_ref[...] = jnp.zeros_like(pair_ref)
    for g in range(3):
        for at, (i, j) in enumerate(PAIRS):
            pair_ref[g, at : at + 1, :] = (
                scaled[i][2 * g : 2 * g + 1] * scaled[j][2 * g + 1 : 2 * g + 2]
            )
    product = None
    for g in range(3):
        whole = pair_ref[g]
        high = whole.astype(bf16)
        rest = whole - high.astype(f32)
        mid = rest.astype(bf16)
        low = (rest - mid.astype(f32)).astype(bf16)
        pieces = jnp.concatenate([high, mid, low], axis=0)
        factor = lax.dot_general(sel_ref[g], pieces, NN, preferred_element_type=f32)
        product = factor if product is None else product * factor
    basis = product * (1.0 / math.sqrt(POSES))
    basis_ref[...] = basis
    stack_ref[0:FIRST, :] = basis[0:FIRST]
    stack_ref[FIRST:STACK, :] = len_ref[...]

    sketch_ids = mus_rank * SKETCH_DEV + lax.broadcasted_iota(i32, (SKETCH_DEV, 1), 0)
    pose_ids = row_rank * POSE_DEV + lax.broadcasted_iota(i32, (1, POSE_DEV), 1)
    row_code = mod_m(3 * mix_round(mod_m(sketch_ids * 389 + seed)))
    pose_code = mod_m(mod_m(pose_ids) * 13 + seed)
    code = row_code + pose_code
    code = jnp.where(code >= modulus, code - modulus, code)
    hashed = mix_round(mix_round(code))
    sketch = ((hashed.astype(f32) + 0.5) * (2.0 / modulus) - 1.0) * math.sqrt(3.0 / SKETCH)
    both = dot3(split2(sketch), split2(stack_ref[...]), NT)
    for r in range(ROWS):
        z_ref[r, :, 0:STACK] = both[8 * r : 8 * r + 8]

    own_ref[...] = jnp.zeros_like(own_ref)
    for k in range(OWN):
        own_ref[k : k + 1, :] = len_ref[pl.ds(mus_rank * OWN + k, 1), :]
    right_ref[0:BLOCK, :] = basis_ref[pl.ds(pl.multiple_of(mus_rank * BLOCK, BLOCK), BLOCK), :]
    right_ref[BLOCK : 2 * BLOCK, :] = own_ref[...]
    columns = dot3(split2(basis), split2(right_ref[...]), NT)
    own = own_ref[...]
    squares = exact(jnp.ones((8, POSE_DEV), f32), own * own, NT)
    for r in range(ROWS):
        for k in range(4):
            at = BLOCK * r + 8 * k
            lane = STACK + BLOCK * k
            z_ref[r, :, lane : lane + BLOCK] = columns[at : at + 8, 0:BLOCK]
            z_ref[r, :, lane + 128 : lane + 128 + BLOCK] = columns[at : at + 8, BLOCK:]
    z_ref[ROWS - 1, :, STACK + 256 - BLOCK : STACK + 256] = squares


def gram_kernel(sc_ref, all_ref, out_ref):
    row_rank = sc_ref[0]
    both = jnp.concatenate([all_ref[r, :, 0:STACK] for r in range(ROWS)], axis=0)
    turned = pltpu.roll(both[:, 0:PAD], lax.rem(PAD - row_rank * BLOCK, PAD), 1)
    block = dot3(split2(turned[:, 0:128]), split2(both), TN)
    out_ref[...] = jnp.zeros_like(out_ref)
    for m in range(MUS):
        for k in range(4):
            rows = block[8 * k : 8 * k + 8]
            lane = BLOCK * k
            muscle = FIRST + OWN * m
            out_ref[m, :, lane : lane + BLOCK] = rows[:, BLOCK * m : BLOCK * m + BLOCK]
            out_ref[m, :, lane + 128 : lane + 128 + OWN] = rows[:, muscle : muscle + OWN]


def place_kernel(sc_ref, tiles_ref, own_ref, out_ref, row_ref):
    for m in range(MUS):
        for k in range(4):
            at = BLOCK * m
            lane = BLOCK * k
            row_ref[8 * k : 8 * k + 8, at : at + BLOCK] = tiles_ref[m, :, lane : lane + BLOCK]
            row_ref[8 * k : 8 * k + 8, PAD + at : PAD + at + BLOCK] = tiles_ref[
                m, :, lane + 128 : lane + 128 + BLOCK
            ]
    half = BLOCK // 2
    core = lax.rem(sc_ref[1], 2)
    out_ref[:, 0 : 2 * PAD] = row_ref[pl.ds(pl.multiple_of(core * half, half), half), :]
    out_ref[0:8, 2 * PAD :] = own_ref[:, 128:256]
    out_ref[8:half, 2 * PAD :] = jnp.zeros((half - 8, 128), f32)


def solve_kernel(
    sc_ref, mine_ref, theirs_ref, all_ref, basis_ref, own_ref, coef_ref, res_ref,
    whole_ref, m_ref, x_ref, e_ref, c_ref, p_ref,
):
    mus_rank = sc_ref[1]
    core = lax.rem(mus_rank, 2)
    half = BLOCK // 2

    def assemble(top_ref, bottom_ref):
        for r in range(ROWS):
            whole_ref[BLOCK * r : BLOCK * r + half, :] = top_ref[r, :, 0 : 2 * PAD]
            whole_ref[BLOCK * r + half : BLOCK * r + BLOCK, :] = bottom_ref[r, :, 0 : 2 * PAD]

    @pl.when(core == 0)
    def _():
        assemble(mine_ref, theirs_ref)

    @pl.when(core == 1)
    def _():
        assemble(theirs_ref, mine_ref)

    rows = lax.broadcasted_iota(i32, (PAD, PAD), 0)
    cols = lax.broadcasted_iota(i32, (PAD, PAD), 1)
    unit = (rows == cols).astype(f32)
    inside = (rows < TERMS) & (cols < TERMS)
    m_ref[...] = jnp.where(inside, whole_ref[:, 0:PAD], unit)
    c_ref[...] = jnp.zeros_like(c_ref)
    p_ref[...] = jnp.zeros_like(p_ref)
    for r in range(ROWS):
        for k in range(4):
            at = BLOCK * r + 8 * k
            lane = BLOCK * k
            c_ref[at : at + 8, 0:BLOCK] = all_ref[
                r, :, STACK + 128 + lane : STACK + 128 + lane + BLOCK
            ]
            p_ref[at : at + 8, 0:BLOCK] = mine_ref[
                r, 0:8, 2 * PAD + lane : 2 * PAD + lane + BLOCK
            ]
    c_all = c_ref[...]
    lengths2 = c_all[PAD - 1 : PAD, :]
    valid = lax.broadcasted_iota(i32, (PAD, 128), 0) < TERMS
    c_own = jnp.where(valid, c_all, 0.0)
    projected = jnp.where(valid, p_ref[...], 0.0)

    def plain(a, b):
        return lax.dot_general(a.astype(bf16), b.astype(bf16), NN, preferred_element_type=f32)

    gram = m_ref[...]
    frob = 1.0 / jnp.sqrt(jnp.sum(gram * gram))
    normed = gram * frob
    square = plain(normed, normed)
    fourth = plain(square, square)
    bound = jnp.sqrt(jnp.sqrt(jnp.sqrt(jnp.sum(fourth * fourth))))
    x_ref[...] = unit * (1.84 * frob / bound)

    def coarse(_, carry):
        x = x_ref[...]
        e = unit - plain(m_ref[...], x)
        x_ref[...] = x + plain(x, e)
        return carry

    lax.fori_loop(0, 5, coarse, 0)

    def fine(state):
        step, _ = state
        x = x_ref[...]
        e = unit - exact(m_ref[...], x, NN)
        x_ref[...] = x + plain(x, e)
        return step + 1, jnp.sum(e * e)

    lax.while_loop(lambda s: (s[0] < 40) & (s[1] > 1e-6), fine, (0, jnp.float32(1.0)))

    inv = functools.partial(lambda b: exact(x_ref[...], b, NN))
    e_ref[...] = jnp.where(inside, whole_ref[:, PAD : 2 * PAD], 0.0)
    apply_g = functools.partial(lambda b: exact(e_ref[...], b, NN))

    def total(a):
        return jnp.sum(a, axis=0, keepdims=True)

    start = inv(projected)
    g_start = apply_g(start)
    g_hat = c_own - g_start
    fresh2 = jnp.maximum(lengths2 - total(start * (c_own + g_hat)), 0.0)
    u_norm = jnp.sqrt(fresh2 + epsilon)
    g_hat = g_hat / u_norm
    u_square = fresh2 / (fresh2 + epsilon)
    t = inv(g_hat)
    v_norm = jnp.sqrt(jnp.maximum(total(g_hat * t), 0.0) + epsilon)
    v_hat = g_hat / v_norm
    t = t / v_norm
    w = t
    phi_bar = u_norm
    rot_bar = v_norm
    y = jnp.zeros_like(t)
    for step in range(ITERS):
        g_t = apply_g(t)
        fresh2 = jnp.maximum(
            total(t * (g_t - 2.0 * v_norm * g_hat)) + v_norm * v_norm * u_square, 0.0
        )
        u_norm = jnp.sqrt(fresh2 + epsilon)
        rot_norm = jnp.sqrt(rot_bar * rot_bar + u_norm * u_norm)
        cosine = rot_bar / rot_norm
        sine = u_norm / rot_norm
        y = y + (cosine * phi_bar / rot_norm) * w
        if step == ITERS - 1:
            break
        g_hat = (g_t - v_norm * g_hat) / u_norm
        u_square = fresh2 / (fresh2 + epsilon)
        q_hat = g_hat - u_norm * v_hat
        t = inv(q_hat)
        v_norm = jnp.sqrt(jnp.maximum(total(q_hat * t), 0.0) + epsilon)
        v_hat = q_hat / v_norm
        t = t / v_norm
        w = t - (sine * v_norm / rot_norm) * w
        rot_bar = -cosine * v_norm
        phi_bar = sine * phi_bar
    coef = jnp.transpose(start + y)
    coef_ref[...] = coef[0:OWN, 0:TERMS]
    fitted = exact(coef[0:BLOCK], basis_ref[...], NN)
    res_ref[...] = own_ref[0:OWN, :] - fitted[0:OWN]


def vmem():
    return pl.BlockSpec(memory_space=pltpu.VMEM)


def smem():
    return pl.BlockSpec(memory_space=pltpu.SMEM)


def per_device(sketch_seed, angles, lengths):
    row_rank = lax.axis_index("rows")
    mus_rank = lax.axis_index("mus")
    ranks = jnp.stack([row_rank, mus_rank, sketch_seed[0]]).astype(i32)
    selectors = jnp.asarray(pair_selectors(), dtype=bf16)

    z, basis, own = pl.pallas_call(
        local_kernel,
        out_shape=(
            jax.ShapeDtypeStruct((ROWS, 8, STACK + 256), f32),
            jax.ShapeDtypeStruct((PAD, POSE_DEV), f32),
            jax.ShapeDtypeStruct((BLOCK, POSE_DEV), f32),
        ),
        in_specs=[smem(), vmem(), vmem(), vmem()],
        out_specs=(vmem(), vmem(), vmem()),
        scratch_shapes=[
            pltpu.VMEM((3, PAIR, POSE_DEV), f32),
            pltpu.VMEM((STACK, POSE_DEV), f32),
            pltpu.VMEM((2 * BLOCK, POSE_DEV), f32),
        ],
        name="local_products",
    )(ranks, angles, lengths, selectors)

    summed = jnp.sum(lax.all_to_all(z, "rows", 0, 0), axis=0)
    everyone = lax.all_to_all(
        jnp.broadcast_to(summed[None], (ROWS,) + summed.shape), "rows", 0, 0
    )

    parts = pl.pallas_call(
        gram_kernel,
        out_shape=jax.ShapeDtypeStruct((MUS, 8, 256), f32),
        in_specs=[smem(), vmem()],
        out_specs=vmem(),
        name="gram_block",
    )(ranks, everyone)
    tile = jnp.sum(lax.all_to_all(parts, "mus", 0, 0), axis=0)
    send = jnp.concatenate([tile[:, 0:128], summed[:, STACK : STACK + 128]], axis=1)
    tiles = lax.all_to_all(jnp.broadcast_to(send[None], (MUS,) + send.shape), "mus", 0, 0)

    half = BLOCK // 2
    kept = pl.pallas_call(
        place_kernel,
        out_shape=jax.ShapeDtypeStruct((half, 2 * PAD + 128), f32),
        in_specs=[smem(), vmem(), vmem()],
        out_specs=vmem(),
        scratch_shapes=[pltpu.VMEM((BLOCK, 2 * PAD), f32)],
        name="place_rows",
    )(ranks, tiles, tile)
    mine = lax.all_to_all(jnp.broadcast_to(kept[None], (ROWS,) + kept.shape), "rows", 0, 0)
    theirs = lax.ppermute(mine, "mus", [(i, i ^ 1) for i in range(MUS)])

    coef, residual = pl.pallas_call(
        solve_kernel,
        out_shape=(
            jax.ShapeDtypeStruct((OWN, TERMS), f32),
            jax.ShapeDtypeStruct((OWN, POSE_DEV), f32),
        ),
        in_specs=[smem()] + [vmem()] * 5,
        out_specs=(vmem(), vmem()),
        scratch_shapes=[
            pltpu.VMEM((PAD, 2 * PAD), f32),
            pltpu.VMEM((PAD, PAD), f32),
            pltpu.VMEM((PAD, PAD), f32),
            pltpu.VMEM((PAD, PAD), f32),
            pltpu.VMEM((PAD, 128), f32),
            pltpu.VMEM((PAD, 128), f32),
        ],
        name="solve",
    )(ranks, mine, theirs, everyone, basis, own)
    return coef, residual


def solution(mesh):
    placed = (P(), P(None, "rows"), P(None, "rows"))
    return jax.shard_map(
        per_device,
        mesh=mesh,
        in_specs=placed,
        out_specs=(P("mus", None), P("mus", "rows")),
        check_vma=False,
    )
```

```python
import functools
import math

import jax
import jax.numpy as jnp
import numpy as np
from jax import lax
from jax.experimental import pallas as pl
from jax.experimental.pallas import tpu as pltpu
from jax.sharding import PartitionSpec as P

ANGLES = 6
DEGREE = 5
TERMS = 462
MUSCLES = 304
SKETCH = 2048
GRID = 64
ITERS = 3
POSES = 12288

ROWS = 16
MUS = 16
POSE_DEV = POSES // ROWS
OWN = MUSCLES // MUS
SKETCH_DEV = SKETCH // MUS
PAD = 512
FIRST = 464
STACK = FIRST + MUSCLES
BLOCK = PAD // ROWS
PAIR = 32

modulus = 46337
epsilon = 1e-06

f32, bf16, i32 = jnp.float32, jnp.bfloat16, jnp.int32
HIGHEST = lax.Precision.HIGHEST
NN = (((1,), (0,)), ((), ()))
NT = (((1,), (1,)), ((), ()))
TN = (((0,), (0,)), ((), ()))


def exponent_table():
    tuples = [[]]
    for angle in range(ANGLES):
        tuples = [
            prefix + [order]
            for prefix in tuples
            for order in range(DEGREE + 1)
            if sum(prefix) + order <= DEGREE
        ]
    return tuples


PAIRS = [(i, j) for i in range(DEGREE + 1) for j in range(DEGREE + 1 - i)]


def pair_selectors():
    table = np.zeros((3, PAD, 3 * PAIR), np.float32)
    for j, entry in enumerate(exponent_table()):
        for g in range(3):
            at = PAIRS.index((entry[2 * g], entry[2 * g + 1]))
            for piece in range(3):
                table[g, j, piece * PAIR + at] = 1.0
    return table


def split2(x):
    high = x.astype(bf16)
    return high, (x - high.astype(f32)).astype(bf16)


def dot3(a, b, dims):
    (ah, al), (bh, bl) = a, b
    one = functools.partial(lax.dot_general, dimension_numbers=dims, preferred_element_type=f32)
    return one(ah, bh) + (one(ah, bl) + one(al, bh))


def exact(a, b, dims):
    return lax.dot_general(a, b, dims, precision=HIGHEST, preferred_element_type=f32)


def mod_m(x):
    quotient = (x.astype(f32) * (1.0 / modulus) - 0.01).astype(i32)
    rest = x - quotient * modulus
    return jnp.where(rest >= modulus, rest - modulus, rest)


def mix_round(x):
    return mod_m(x * x + 7919)


def local_kernel(sc_ref, ang_ref, len_ref, sel_ref, z_ref, basis_ref, own_ref, pair_ref, stack_ref, right_ref):
    row_rank, mus_rank, seed = sc_ref[0], sc_ref[1], sc_ref[2]
    position = (2.0 * ang_ref[...].astype(f32) + 1.0) / GRID - 1.0
    plain = [jnp.ones_like(position), position]
    for order in range(1, DEGREE):
        plain.append(
            ((2 * order + 1) * position * plain[order] - order * plain[order - 1])
            * (1.0 / (order + 1))
        )
    scaled = [math.sqrt(2 * order + 1) * plain[order] for order in range(DEGREE + 1)]
    pair_ref[...] = jnp.zeros_like(pair_ref)
    for g in range(3):
        for at, (i, j) in enumerate(PAIRS):
            pair_ref[g, at : at + 1, :] = (
                scaled[i][2 * g : 2 * g + 1] * scaled[j][2 * g + 1 : 2 * g + 2]
            )
    product = None
    for g in range(3):
        whole = pair_ref[g]
        high = whole.astype(bf16)
        rest = whole - high.astype(f32)
        mid = rest.astype(bf16)
        low = (rest - mid.astype(f32)).astype(bf16)
        pieces = jnp.concatenate([high, mid, low], axis=0)
        factor = lax.dot_general(sel_ref[g], pieces, NN, preferred_element_type=f32)
        product = factor if product is None else product * factor
    basis = product * (1.0 / math.sqrt(POSES))
    basis_ref[...] = basis
    stack_ref[0:FIRST, :] = basis[0:FIRST]
    stack_ref[FIRST:STACK, :] = len_ref[...]

    sketch_ids = mus_rank * SKETCH_DEV + lax.broadcasted_iota(i32, (SKETCH_DEV, 1), 0)
    pose_ids = row_rank * POSE_DEV + lax.broadcasted_iota(i32, (1, POSE_DEV), 1)
    row_code = mod_m(3 * mix_round(mod_m(sketch_ids * 389 + seed)))
    pose_code = mod_m(mod_m(pose_ids) * 13 + seed)
    code = row_code + pose_code
    code = jnp.where(code >= modulus, code - modulus, code)
    hashed = mix_round(mix_round(code))
    sketch = ((hashed.astype(f32) + 0.5) * (2.0 / modulus) - 1.0) * math.sqrt(3.0 / SKETCH)
    both = dot3(split2(sketch), split2(stack_ref[...]), NT)
    for r in range(ROWS):
        z_ref[r, :, 0:STACK] = both[8 * r : 8 * r + 8]

    own_ref[...] = jnp.zeros_like(own_ref)
    for k in range(OWN):
        own_ref[k : k + 1, :] = len_ref[pl.ds(mus_rank * OWN + k, 1), :]
    right_ref[0:BLOCK, :] = basis_ref[pl.ds(pl.multiple_of(mus_rank * BLOCK, BLOCK), BLOCK), :]
    right_ref[BLOCK : 2 * BLOCK, :] = own_ref[...]
    columns = dot3(split2(basis), split2(right_ref[...]), NT)
    own = own_ref[...]
    squares = exact(jnp.ones((8, POSE_DEV), f32), own * own, NT)
    for r in range(ROWS):
        for k in range(4):
            at = BLOCK * r + 8 * k
            lane = STACK + BLOCK * k
            z_ref[r, :, lane : lane + BLOCK] = columns[at : at + 8, 0:BLOCK]
            z_ref[r, :, lane + 128 : lane + 128 + BLOCK] = columns[at : at + 8, BLOCK:]
    z_ref[ROWS - 1, :, STACK + 256 - BLOCK : STACK + 256] = squares


def gram_kernel(sc_ref, all_ref, out_ref):
    row_rank = sc_ref[0]
    both = jnp.concatenate([all_ref[r, :, 0:STACK] for r in range(ROWS)], axis=0)
    turned = pltpu.roll(both[:, 0:PAD], lax.rem(PAD - row_rank * BLOCK, PAD), 1)
    block = dot3(split2(turned[:, 0:128]), split2(both), TN)
    out_ref[...] = jnp.zeros_like(out_ref)
    for m in range(MUS):
        for k in range(4):
            rows = block[8 * k : 8 * k + 8]
            lane = BLOCK * k
            muscle = FIRST + OWN * m
            out_ref[m, :, lane : lane + BLOCK] = rows[:, BLOCK * m : BLOCK * m + BLOCK]
            out_ref[m, :, lane + 128 : lane + 128 + OWN] = rows[:, muscle : muscle + OWN]


def place_kernel(sc_ref, tiles_ref, own_ref, out_ref, row_ref):
    for m in range(MUS):
        for k in range(4):
            at = BLOCK * m
            lane = BLOCK * k
            row_ref[8 * k : 8 * k + 8, at : at + BLOCK] = tiles_ref[m, :, lane : lane + BLOCK]
            row_ref[8 * k : 8 * k + 8, PAD + at : PAD + at + BLOCK] = tiles_ref[
                m, :, lane + 128 : lane + 128 + BLOCK
            ]
    half = BLOCK // 2
    core = lax.rem(sc_ref[1], 2)
    out_ref[:, 0 : 2 * PAD] = row_ref[pl.ds(pl.multiple_of(core * half, half), half), :]
    out_ref[0:8, 2 * PAD :] = own_ref[:, 128:256]
    out_ref[8:half, 2 * PAD :] = jnp.zeros((half - 8, 128), f32)


def solve_kernel(
    sc_ref, mine_ref, theirs_ref, all_ref, basis_ref, own_ref, coef_ref, res_ref,
    whole_ref, x_ref, mh_ref, ml_ref, xh_ref, xl_ref, gh_ref, gl_ref, c_ref, p_ref,
):
    mus_rank = sc_ref[1]
    core = lax.rem(mus_rank, 2)
    half = BLOCK // 2

    def assemble(top_ref, bottom_ref):
        for r in range(ROWS):
            whole_ref[BLOCK * r : BLOCK * r + half, :] = top_ref[r, :, 0 : 2 * PAD]
            whole_ref[BLOCK * r + half : BLOCK * r + BLOCK, :] = bottom_ref[r, :, 0 : 2 * PAD]

    @pl.when(core == 0)
    def _():
        assemble(mine_ref, theirs_ref)

    @pl.when(core == 1)
    def _():
        assemble(theirs_ref, mine_ref)

    rows = lax.broadcasted_iota(i32, (PAD, PAD), 0)
    cols = lax.broadcasted_iota(i32, (PAD, PAD), 1)
    unit = (rows == cols).astype(f32)
    inside = (rows < TERMS) & (cols < TERMS)
    gram = jnp.where(inside, whole_ref[:, 0:PAD], unit)
    mh_ref[...], ml_ref[...] = split2(gram)
    gh_ref[...], gl_ref[...] = split2(jnp.where(inside, whole_ref[:, PAD : 2 * PAD], 0.0))
    c_ref[...] = jnp.zeros_like(c_ref)
    p_ref[...] = jnp.zeros_like(p_ref)
    for r in range(ROWS):
        for k in range(4):
            at = BLOCK * r + 8 * k
            lane = BLOCK * k
            c_ref[at : at + 8, 0:BLOCK] = all_ref[
                r, :, STACK + 128 + lane : STACK + 128 + lane + BLOCK
            ]
            p_ref[at : at + 8, 0:BLOCK] = mine_ref[
                r, 0:8, 2 * PAD + lane : 2 * PAD + lane + BLOCK
            ]
    c_all = c_ref[...]
    lengths2 = c_all[PAD - 1 : PAD, :]
    valid = lax.broadcasted_iota(i32, (PAD, 128), 0) < TERMS
    c_own = jnp.where(valid, c_all, 0.0)
    projected = jnp.where(valid, p_ref[...], 0.0)

    def plain(a, b):
        return lax.dot_general(a.astype(bf16), b.astype(bf16), NN, preferred_element_type=f32)

    frob = 1.0 / jnp.sqrt(jnp.sum(gram * gram))
    normed = (gram * frob).astype(bf16)
    square = plain(normed, normed)
    fourth = plain(square, square)
    bound = jnp.sqrt(jnp.sqrt(jnp.sqrt(jnp.sum(fourth * fourth))))
    scale = 1.84 * frob / bound
    x_ref[...] = (2.0 * scale) * unit - (scale * scale) * gram

    def coarse(_, carry):
        x = x_ref[...]
        high = x.astype(bf16)
        e = unit - plain(mh_ref[...], high)
        x_ref[...] = x + plain(high, e)
        return carry

    lax.fori_loop(0, 4, coarse, 0)

    def fine(state):
        step, _ = state
        x = x_ref[...]
        parts = split2(x)
        e = unit - dot3((mh_ref[...], ml_ref[...]), parts, NN)
        x_ref[...] = x + plain(parts[0], e)
        return step + 1, jnp.sum(e * e)

    lax.while_loop(lambda s: (s[0] < 40) & (s[1] > 1e-6), fine, (0, jnp.float32(1.0)))
    xh_ref[...], xl_ref[...] = split2(x_ref[...])

    left = lax.broadcasted_iota(i32, (PAD, 128), 1) < 64

    def times(high_ref, low_ref, b):
        high = b.astype(bf16).astype(f32)
        pieces = jnp.where(left, high, pltpu.roll(b - high, 64, 1)).astype(bf16)
        one = functools.partial(lax.dot_general, dimension_numbers=NN, preferred_element_type=f32)
        product = one(high_ref[...], pieces) + one(low_ref[...], pieces)
        return product + pltpu.roll(product, 64, 1)

    inv = functools.partial(times, xh_ref, xl_ref)
    apply_g = functools.partial(times, gh_ref, gl_ref)

    def total(a):
        return jnp.sum(a, axis=0, keepdims=True)

    start = inv(projected)
    g_start = apply_g(start)
    g_hat = c_own - g_start
    fresh2 = jnp.maximum(lengths2 - total(start * (c_own + g_hat)), 0.0)
    u_norm = jnp.sqrt(fresh2 + epsilon)
    g_hat = g_hat / u_norm
    u_square = fresh2 / (fresh2 + epsilon)
    t = inv(g_hat)
    v_norm = jnp.sqrt(jnp.maximum(total(g_hat * t), 0.0) + epsilon)
    v_hat = g_hat / v_norm
    t = t / v_norm
    w = t
    phi_bar = u_norm
    rot_bar = v_norm
    y = jnp.zeros_like(t)
    for step in range(ITERS):
        g_t = apply_g(t)
        fresh2 = jnp.maximum(
            total(t * (g_t - 2.0 * v_norm * g_hat)) + v_norm * v_norm * u_square, 0.0
        )
        u_norm = jnp.sqrt(fresh2 + epsilon)
        rot_norm = jnp.sqrt(rot_bar * rot_bar + u_norm * u_norm)
        cosine = rot_bar / rot_norm
        sine = u_norm / rot_norm
        y = y + (cosine * phi_bar / rot_norm) * w
        if step == ITERS - 1:
            break
        g_hat = (g_t - v_norm * g_hat) / u_norm
        u_square = fresh2 / (fresh2 + epsilon)
        q_hat = g_hat - u_norm * v_hat
        t = inv(q_hat)
        v_norm = jnp.sqrt(jnp.maximum(total(q_hat * t), 0.0) + epsilon)
        v_hat = q_hat / v_norm
        t = t / v_norm
        w = t - (sine * v_norm / rot_norm) * w
        rot_bar = -cosine * v_norm
        phi_bar = sine * phi_bar
    coef = jnp.transpose(start + y)
    coef_ref[...] = coef[0:OWN, 0:TERMS]
    fitted = dot3(split2(coef[0:BLOCK]), split2(basis_ref[...]), NN)
    res_ref[...] = own_ref[0:OWN, :] - fitted[0:OWN]


def vmem():
    return pl.BlockSpec(memory_space=pltpu.VMEM)


def smem():
    return pl.BlockSpec(memory_space=pltpu.SMEM)


def per_device(sketch_seed, angles, lengths):
    row_rank = lax.axis_index("rows")
    mus_rank = lax.axis_index("mus")
    ranks = jnp.stack([row_rank, mus_rank, sketch_seed[0]]).astype(i32)
    selectors = jnp.asarray(pair_selectors(), dtype=bf16)

    z, basis, own = pl.pallas_call(
        local_kernel,
        out_shape=(
            jax.ShapeDtypeStruct((ROWS, 8, STACK + 256), f32),
            jax.ShapeDtypeStruct((PAD, POSE_DEV), f32),
            jax.ShapeDtypeStruct((BLOCK, POSE_DEV), f32),
        ),
        in_specs=[smem(), vmem(), vmem(), vmem()],
        out_specs=(vmem(), vmem(), vmem()),
        scratch_shapes=[
            pltpu.VMEM((3, PAIR, POSE_DEV), f32),
            pltpu.VMEM((STACK, POSE_DEV), f32),
            pltpu.VMEM((2 * BLOCK, POSE_DEV), f32),
        ],
        name="local_products",
    )(ranks, angles, lengths, selectors)

    summed = jnp.sum(lax.all_to_all(z, "rows", 0, 0), axis=0)
    everyone = lax.all_to_all(
        jnp.broadcast_to(summed[None], (ROWS,) + summed.shape), "rows", 0, 0
    )

    parts = pl.pallas_call(
        gram_kernel,
        out_shape=jax.ShapeDtypeStruct((MUS, 8, 256), f32),
        in_specs=[smem(), vmem()],
        out_specs=vmem(),
        name="gram_block",
    )(ranks, everyone)
    tile = jnp.sum(lax.all_to_all(parts, "mus", 0, 0), axis=0)
    send = jnp.concatenate([tile[:, 0:128], summed[:, STACK : STACK + 128]], axis=1)
    tiles = lax.all_to_all(jnp.broadcast_to(send[None], (MUS,) + send.shape), "mus", 0, 0)

    half = BLOCK // 2
    kept = pl.pallas_call(
        place_kernel,
        out_shape=jax.ShapeDtypeStruct((half, 2 * PAD + 128), f32),
        in_specs=[smem(), vmem(), vmem()],
        out_specs=vmem(),
        scratch_shapes=[pltpu.VMEM((BLOCK, 2 * PAD), f32)],
        name="place_rows",
    )(ranks, tiles, tile)
    mine = lax.all_to_all(jnp.broadcast_to(kept[None], (ROWS,) + kept.shape), "rows", 0, 0)
    theirs = lax.ppermute(mine, "mus", [(i, i ^ 1) for i in range(MUS)])

    coef, residual = pl.pallas_call(
        solve_kernel,
        out_shape=(
            jax.ShapeDtypeStruct((OWN, TERMS), f32),
            jax.ShapeDtypeStruct((OWN, POSE_DEV), f32),
        ),
        in_specs=[smem()] + [vmem()] * 5,
        out_specs=(vmem(), vmem()),
        scratch_shapes=[
            pltpu.VMEM((PAD, 2 * PAD), f32),
            pltpu.VMEM((PAD, PAD), f32),
        ]
        + [pltpu.VMEM((PAD, PAD), bf16)] * 6
        + [
            pltpu.VMEM((PAD, 128), f32),
            pltpu.VMEM((PAD, 128), f32),
        ],
        name="solve",
    )(ranks, mine, theirs, everyone, basis, own)
    return coef, residual


def solution(mesh):
    placed = (P(), P(None, "rows"), P(None, "rows"))
    return jax.shard_map(
        per_device,
        mesh=mesh,
        in_specs=placed,
        out_specs=(P("mus", None), P("mus", "rows")),
        check_vma=False,
    )
```

```python
import functools
import math

import jax
import jax.numpy as jnp
import numpy as np
from jax import lax
from jax.experimental import pallas as pl
from jax.experimental.pallas import tpu as pltpu
from jax.sharding import PartitionSpec as P

ANGLES = 6
DEGREE = 5
TERMS = 462
MUSCLES = 304
SKETCH = 2048
GRID = 64
ITERS = 3
POSES = 12288

ROWS = 16
MUS = 16
POSE_DEV = POSES // ROWS
OWN = MUSCLES // MUS
SKETCH_DEV = SKETCH // MUS
PAD = 512
FIRST = 464
STACK = FIRST + MUSCLES
BLOCK = PAD // ROWS
PAIR = 32

modulus = 46337
epsilon = 1e-06

f32, bf16, i32 = jnp.float32, jnp.bfloat16, jnp.int32
HIGHEST = lax.Precision.HIGHEST
NN = (((1,), (0,)), ((), ()))
NT = (((1,), (1,)), ((), ()))
TN = (((0,), (0,)), ((), ()))


def exponent_table():
    tuples = [[]]
    for angle in range(ANGLES):
        tuples = [
            prefix + [order]
            for prefix in tuples
            for order in range(DEGREE + 1)
            if sum(prefix) + order <= DEGREE
        ]
    return tuples


PAIRS = [(i, j) for i in range(DEGREE + 1) for j in range(DEGREE + 1 - i)]


def pair_selectors():
    table = np.zeros((3, PAD, 3 * PAIR), np.float32)
    for j, entry in enumerate(exponent_table()):
        for g in range(3):
            at = PAIRS.index((entry[2 * g], entry[2 * g + 1]))
            for piece in range(3):
                table[g, j, piece * PAIR + at] = 1.0
    return table


def split2(x):
    high = x.astype(bf16)
    return high, (x - high.astype(f32)).astype(bf16)


def dot3(a, b, dims):
    (ah, al), (bh, bl) = a, b
    one = functools.partial(lax.dot_general, dimension_numbers=dims, preferred_element_type=f32)
    return one(ah, bh) + (one(ah, bl) + one(al, bh))


def exact(a, b, dims):
    return lax.dot_general(a, b, dims, precision=HIGHEST, preferred_element_type=f32)


def mod_m(x):
    quotient = (x.astype(f32) * (1.0 / modulus) - 0.01).astype(i32)
    rest = x - quotient * modulus
    return jnp.where(rest >= modulus, rest - modulus, rest)


def mix_round(x):
    return mod_m(x * x + 7919)


def local_kernel(seed_ref, ang_ref, len_ref, sel_ref, z_ref, basis_ref, own_ref, pair_ref, stack_ref, right_ref):
    row_rank, mus_rank, seed = lax.axis_index("rows"), lax.axis_index("mus"), seed_ref[0]
    position = (2.0 * ang_ref[...].astype(f32) + 1.0) / GRID - 1.0
    plain = [jnp.ones_like(position), position]
    for order in range(1, DEGREE):
        plain.append(
            ((2 * order + 1) * position * plain[order] - order * plain[order - 1])
            * (1.0 / (order + 1))
        )
    scaled = [math.sqrt(2 * order + 1) * plain[order] for order in range(DEGREE + 1)]
    pair_ref[...] = jnp.zeros_like(pair_ref)
    for g in range(3):
        for at, (i, j) in enumerate(PAIRS):
            pair_ref[g, at : at + 1, :] = (
                scaled[i][2 * g : 2 * g + 1] * scaled[j][2 * g + 1 : 2 * g + 2]
            )
    product = None
    for g in range(3):
        whole = pair_ref[g]
        high = whole.astype(bf16)
        rest = whole - high.astype(f32)
        mid = rest.astype(bf16)
        low = (rest - mid.astype(f32)).astype(bf16)
        pieces = jnp.concatenate([high, mid, low], axis=0)
        factor = lax.dot_general(sel_ref[g], pieces, NN, preferred_element_type=f32)
        product = factor if product is None else product * factor
    basis = product * (1.0 / math.sqrt(POSES))
    basis_ref[...] = basis
    stack_ref[0:FIRST, :] = basis[0:FIRST]
    stack_ref[FIRST:STACK, :] = len_ref[...]

    sketch_ids = mus_rank * SKETCH_DEV + lax.broadcasted_iota(i32, (SKETCH_DEV, 1), 0)
    pose_ids = row_rank * POSE_DEV + lax.broadcasted_iota(i32, (1, POSE_DEV), 1)
    row_code = mod_m(3 * mix_round(mod_m(sketch_ids * 389 + seed)))
    pose_code = mod_m(mod_m(pose_ids) * 13 + seed)
    code = row_code + pose_code
    code = jnp.where(code >= modulus, code - modulus, code)
    hashed = mix_round(mix_round(code))
    sketch = ((hashed.astype(f32) + 0.5) * (2.0 / modulus) - 1.0) * math.sqrt(3.0 / SKETCH)
    both = dot3(split2(sketch), split2(stack_ref[...]), NT)
    for r in range(ROWS):
        z_ref[r, :, 0:STACK] = both[8 * r : 8 * r + 8]

    own_ref[...] = jnp.zeros_like(own_ref)
    for k in range(OWN):
        own_ref[k : k + 1, :] = len_ref[pl.ds(mus_rank * OWN + k, 1), :]
    right_ref[0:BLOCK, :] = basis_ref[pl.ds(pl.multiple_of(mus_rank * BLOCK, BLOCK), BLOCK), :]
    right_ref[BLOCK : 2 * BLOCK, :] = own_ref[...]
    columns = dot3(split2(basis), split2(right_ref[...]), NT)
    own = own_ref[...]
    squares = exact(jnp.ones((8, POSE_DEV), f32), own * own, NT)
    for r in range(ROWS):
        for k in range(4):
            at = BLOCK * r + 8 * k
            lane = STACK + BLOCK * k
            z_ref[r, :, lane : lane + BLOCK] = columns[at : at + 8, 0:BLOCK]
            z_ref[r, :, lane + 128 : lane + 128 + BLOCK] = columns[at : at + 8, BLOCK:]
    z_ref[ROWS - 1, :, STACK + 256 - BLOCK : STACK + 256] = squares


def gram_kernel(all_ref, out_ref):
    row_rank = lax.axis_index("rows")
    both = jnp.concatenate([all_ref[r, :, 0:STACK] for r in range(ROWS)], axis=0)
    turned = pltpu.roll(both[:, 0:PAD], lax.rem(PAD - row_rank * BLOCK, PAD), 1)
    block = dot3(split2(turned[:, 0:128]), split2(both), TN)
    out_ref[...] = jnp.zeros_like(out_ref)
    for m in range(MUS):
        for k in range(4):
            rows = block[8 * k : 8 * k + 8]
            lane = BLOCK * k
            muscle = FIRST + OWN * m
            out_ref[m, :, lane : lane + BLOCK] = rows[:, BLOCK * m : BLOCK * m + BLOCK]
            out_ref[m, :, lane + 128 : lane + 128 + OWN] = rows[:, muscle : muscle + OWN]


def place_kernel(tiles_ref, own_ref, out_ref, row_ref):
    for m in range(MUS):
        for k in range(4):
            at = BLOCK * m
            lane = BLOCK * k
            row_ref[8 * k : 8 * k + 8, at : at + BLOCK] = tiles_ref[m, :, lane : lane + BLOCK]
            row_ref[8 * k : 8 * k + 8, PAD + at : PAD + at + BLOCK] = tiles_ref[
                m, :, lane + 128 : lane + 128 + BLOCK
            ]
    half = BLOCK // 2
    core = lax.rem(lax.axis_index("mus"), 2)
    kept = row_ref[pl.ds(pl.multiple_of(core * half, half), half), :]
    for r in range(ROWS):
        out_ref[r, :, 0 : 2 * PAD] = kept
        out_ref[r, 0:8, 2 * PAD :] = own_ref[:, 128:256]
        out_ref[r, 8:half, 2 * PAD :] = jnp.zeros((half - 8, 128), f32)


def solve_kernel(
    mine_ref, theirs_ref, all_ref, basis_hbm, own_ref, coef_ref, res_ref,
    whole_ref, x_ref, mh_ref, ml_ref, xh_ref, xl_ref, gh_ref, gl_ref, c_ref, p_ref, basis_ref, sem,
):
    fetch = pltpu.make_async_copy(basis_hbm, basis_ref, sem)
    fetch.start()
    core = lax.rem(lax.axis_index("mus"), 2)
    half = BLOCK // 2

    def assemble(top_ref, bottom_ref):
        for r in range(ROWS):
            whole_ref[BLOCK * r : BLOCK * r + half, :] = top_ref[r, :, 0 : 2 * PAD]
            whole_ref[BLOCK * r + half : BLOCK * r + BLOCK, :] = bottom_ref[r, :, 0 : 2 * PAD]

    @pl.when(core == 0)
    def _():
        assemble(mine_ref, theirs_ref)

    @pl.when(core == 1)
    def _():
        assemble(theirs_ref, mine_ref)

    rows = lax.broadcasted_iota(i32, (PAD, PAD), 0)
    cols = lax.broadcasted_iota(i32, (PAD, PAD), 1)
    unit = (rows == cols).astype(f32)
    inside = (rows < TERMS) & (cols < TERMS)
    gram = jnp.where(inside, whole_ref[:, 0:PAD], unit)
    mh_ref[...], ml_ref[...] = split2(gram)
    gh_ref[...], gl_ref[...] = split2(jnp.where(inside, whole_ref[:, PAD : 2 * PAD], 0.0))
    c_ref[...] = jnp.zeros_like(c_ref)
    p_ref[...] = jnp.zeros_like(p_ref)
    for r in range(ROWS):
        for k in range(4):
            at = BLOCK * r + 8 * k
            lane = BLOCK * k
            c_ref[at : at + 8, 0:BLOCK] = all_ref[
                r, :, STACK + lane : STACK + lane + BLOCK
            ]
            p_ref[at : at + 8, 0:BLOCK] = mine_ref[
                r, 0:8, 2 * PAD + lane : 2 * PAD + lane + BLOCK
            ]
    c_all = c_ref[...]
    lengths2 = c_all[PAD - 1 : PAD, :]
    valid = lax.broadcasted_iota(i32, (PAD, 128), 0) < TERMS
    c_own = jnp.where(valid, c_all, 0.0)
    projected = jnp.where(valid, p_ref[...], 0.0)

    def plain(a, b):
        return lax.dot_general(a.astype(bf16), b.astype(bf16), NN, preferred_element_type=f32)

    frob = 1.0 / jnp.sqrt(jnp.sum(gram * gram))
    normed = (gram * frob).astype(bf16)
    square = plain(normed, normed)
    fourth = plain(square, square)
    bound = jnp.sqrt(jnp.sqrt(jnp.sqrt(jnp.sum(fourth * fourth))))
    scale = 1.84 * frob / bound
    x_ref[...] = (2.0 * scale) * unit - (scale * scale) * gram

    def coarse(_, carry):
        x = x_ref[...]
        high = x.astype(bf16)
        e = unit - plain(mh_ref[...], high)
        x_ref[...] = x + plain(high, e)
        return carry

    lax.fori_loop(0, 4, coarse, 0)

    def fine(state):
        step, _ = state
        x = x_ref[...]
        parts = split2(x)
        e = unit - dot3((mh_ref[...], ml_ref[...]), parts, NN)
        x_ref[...] = x + plain(parts[0], e)
        return step + 1, jnp.sum(e * e)

    lax.while_loop(lambda s: (s[0] < 40) & (s[1] > 1e-6), fine, (0, jnp.float32(1.0)))
    xh_ref[...], xl_ref[...] = split2(x_ref[...])

    left = lax.broadcasted_iota(i32, (PAD, 128), 1) < 64

    def times(high_ref, low_ref, b):
        high = b.astype(bf16).astype(f32)
        pieces = jnp.where(left, high, pltpu.roll(b - high, 64, 1)).astype(bf16)
        one = functools.partial(lax.dot_general, dimension_numbers=NN, preferred_element_type=f32)
        product = one(high_ref[...], pieces) + one(low_ref[...], pieces)
        return product + pltpu.roll(product, 64, 1)

    inv = functools.partial(times, xh_ref, xl_ref)
    apply_g = functools.partial(times, gh_ref, gl_ref)

    def total(a):
        return jnp.sum(a, axis=0, keepdims=True)

    start = inv(projected)
    g_start = apply_g(start)
    g_hat = c_own - g_start
    fresh2 = jnp.maximum(lengths2 - total(start * (c_own + g_hat)), 0.0)
    u_norm = jnp.sqrt(fresh2 + epsilon)
    g_hat = g_hat / u_norm
    u_square = fresh2 / (fresh2 + epsilon)
    t = inv(g_hat)
    v_norm = jnp.sqrt(jnp.maximum(total(g_hat * t), 0.0) + epsilon)
    v_hat = g_hat / v_norm
    t = t / v_norm
    w = t
    phi_bar = u_norm
    rot_bar = v_norm
    y = jnp.zeros_like(t)
    for step in range(ITERS):
        g_t = apply_g(t)
        fresh2 = jnp.maximum(
            total(t * (g_t - 2.0 * v_norm * g_hat)) + v_norm * v_norm * u_square, 0.0
        )
        u_norm = jnp.sqrt(fresh2 + epsilon)
        rot_norm = jnp.sqrt(rot_bar * rot_bar + u_norm * u_norm)
        cosine = rot_bar / rot_norm
        sine = u_norm / rot_norm
        y = y + (cosine * phi_bar / rot_norm) * w
        if step == ITERS - 1:
            break
        g_hat = (g_t - v_norm * g_hat) / u_norm
        u_square = fresh2 / (fresh2 + epsilon)
        q_hat = g_hat - u_norm * v_hat
        t = inv(q_hat)
        v_norm = jnp.sqrt(jnp.maximum(total(q_hat * t), 0.0) + epsilon)
        v_hat = q_hat / v_norm
        t = t / v_norm
        w = t - (sine * v_norm / rot_norm) * w
        rot_bar = -cosine * v_norm
        phi_bar = sine * phi_bar
    coef = jnp.transpose(start + y)
    coef_ref[...] = coef[0:OWN, 0:TERMS]
    fetch.wait()
    fitted = dot3(split2(coef[0:BLOCK]), split2(basis_ref[...]), NN)
    res_ref[...] = own_ref[0:OWN, :] - fitted[0:OWN]


def vmem():
    return pl.BlockSpec(memory_space=pltpu.VMEM)


def smem():
    return pl.BlockSpec(memory_space=pltpu.SMEM)


def per_device(sketch_seed, angles, lengths):
    selectors = jnp.asarray(pair_selectors(), dtype=bf16)

    z, basis, own = pl.pallas_call(
        local_kernel,
        out_shape=(
            jax.ShapeDtypeStruct((ROWS, 8, STACK + 256), f32),
            jax.ShapeDtypeStruct((PAD, POSE_DEV), f32),
            jax.ShapeDtypeStruct((BLOCK, POSE_DEV), f32),
        ),
        in_specs=[smem(), vmem(), vmem(), vmem()],
        out_specs=(vmem(), vmem(), vmem()),
        scratch_shapes=[
            pltpu.VMEM((3, PAIR, POSE_DEV), f32),
            pltpu.VMEM((STACK, POSE_DEV), f32),
            pltpu.VMEM((2 * BLOCK, POSE_DEV), f32),
        ],
        name="local_products",
    )(sketch_seed, angles, lengths, selectors)

    summed = jnp.sum(lax.all_to_all(z, "rows", 0, 0), axis=0)
    shared = jnp.concatenate([summed[:, 0:STACK], summed[:, STACK + 128 :]], axis=1)
    everyone = lax.all_to_all(
        jnp.broadcast_to(shared[None], (ROWS,) + shared.shape), "rows", 0, 0
    )

    parts = pl.pallas_call(
        gram_kernel,
        out_shape=jax.ShapeDtypeStruct((MUS, 8, 256), f32),
        in_specs=[vmem()],
        out_specs=vmem(),
        name="gram_block",
    )(everyone)
    tile = jnp.sum(lax.all_to_all(parts, "mus", 0, 0), axis=0)
    send = jnp.concatenate([tile[:, 0:128], summed[:, STACK : STACK + 128]], axis=1)
    tiles = lax.all_to_all(jnp.broadcast_to(send[None], (MUS,) + send.shape), "mus", 0, 0)

    half = BLOCK // 2
    kept = pl.pallas_call(
        place_kernel,
        out_shape=jax.ShapeDtypeStruct((ROWS, half, 2 * PAD + 128), f32),
        in_specs=[vmem(), vmem()],
        out_specs=vmem(),
        scratch_shapes=[pltpu.VMEM((BLOCK, 2 * PAD), f32)],
        name="place_rows",
    )(tiles, tile)
    mine = lax.all_to_all(kept, "rows", 0, 0)
    theirs = lax.ppermute(mine, "mus", [(i, i ^ 1) for i in range(MUS)])

    coef, residual = pl.pallas_call(
        solve_kernel,
        out_shape=(
            jax.ShapeDtypeStruct((OWN, TERMS), f32),
            jax.ShapeDtypeStruct((OWN, POSE_DEV), f32),
        ),
        in_specs=[vmem()] * 3 + [pl.BlockSpec(memory_space=pl.ANY), vmem()],
        out_specs=(vmem(), vmem()),
        scratch_shapes=[
            pltpu.VMEM((PAD, 2 * PAD), f32),
            pltpu.VMEM((PAD, PAD), f32),
        ]
        + [pltpu.VMEM((PAD, PAD), bf16)] * 6
        + [
            pltpu.VMEM((PAD, 128), f32),
            pltpu.VMEM((PAD, 128), f32),
            pltpu.VMEM((PAD, POSE_DEV), f32),
            pltpu.SemaphoreType.DMA(()),
        ],
        name="solve",
    )(mine, theirs, everyone, basis, own)
    return coef, residual


def solution(mesh):
    placed = (P(), P(None, "rows"), P(None, "rows"))
    return jax.shard_map(
        per_device,
        mesh=mesh,
        in_specs=placed,
        out_specs=(P("mus", None), P("mus", "rows")),
        check_vma=False,
    )
```

```python
import functools
import math

import jax
import jax.numpy as jnp
import numpy as np
from jax import lax
from jax.experimental import pallas as pl
from jax.experimental.pallas import tpu as pltpu
from jax.sharding import PartitionSpec as P

ANGLES = 6
DEGREE = 5
TERMS = 462
MUSCLES = 304
SKETCH = 2048
GRID = 64
ITERS = 3
POSES = 12288

ROWS = 16
MUS = 16
POSE_DEV = POSES // ROWS
OWN = MUSCLES // MUS
SKETCH_DEV = SKETCH // MUS
PAD = 512
FIRST = 464
STACK = FIRST + MUSCLES
BLOCK = PAD // ROWS
PAIR = 32

modulus = 46337
epsilon = 1e-06

f32, bf16, i32 = jnp.float32, jnp.bfloat16, jnp.int32
HIGHEST = lax.Precision.HIGHEST
NN = (((1,), (0,)), ((), ()))
NT = (((1,), (1,)), ((), ()))
TN = (((0,), (0,)), ((), ()))


def exponent_table():
    tuples = [[]]
    for angle in range(ANGLES):
        tuples = [
            prefix + [order]
            for prefix in tuples
            for order in range(DEGREE + 1)
            if sum(prefix) + order <= DEGREE
        ]
    return tuples


PAIRS = [(i, j) for i in range(DEGREE + 1) for j in range(DEGREE + 1 - i)]


def pair_selectors():
    table = np.zeros((3, PAD, 3 * PAIR), np.float32)
    for j, entry in enumerate(exponent_table()):
        for g in range(3):
            at = PAIRS.index((entry[2 * g], entry[2 * g + 1]))
            for piece in range(3):
                table[g, j, piece * PAIR + at] = 1.0
    return table


def split2(x):
    high = x.astype(bf16)
    return high, (x - high.astype(f32)).astype(bf16)


def dot3(a, b, dims):
    (ah, al), (bh, bl) = a, b
    one = functools.partial(lax.dot_general, dimension_numbers=dims, preferred_element_type=f32)
    return one(ah, bh) + (one(ah, bl) + one(al, bh))


def exact(a, b, dims):
    return lax.dot_general(a, b, dims, precision=HIGHEST, preferred_element_type=f32)


def mod_m(x):
    quotient = (x.astype(f32) * (1.0 / modulus) - 0.01).astype(i32)
    rest = x - quotient * modulus
    return jnp.where(rest >= modulus, rest - modulus, rest)


def mix_round(x):
    return mod_m(x * x + 7919)


def local_kernel(seed_ref, ang_ref, len_ref, sel_ref, z_ref, basis_ref, own_ref, pair_ref, stack_ref, right_ref):
    row_rank, mus_rank, seed = lax.axis_index("rows"), lax.axis_index("mus"), seed_ref[0]
    position = (2.0 * ang_ref[...].astype(f32) + 1.0) / GRID - 1.0
    plain = [jnp.ones_like(position), position]
    for order in range(1, DEGREE):
        plain.append(
            ((2 * order + 1) * position * plain[order] - order * plain[order - 1])
            * (1.0 / (order + 1))
        )
    scaled = [math.sqrt(2 * order + 1) * plain[order] for order in range(DEGREE + 1)]
    pair_ref[...] = jnp.zeros_like(pair_ref)
    for g in range(3):
        for at, (i, j) in enumerate(PAIRS):
            pair_ref[g, at : at + 1, :] = (
                scaled[i][2 * g : 2 * g + 1] * scaled[j][2 * g + 1 : 2 * g + 2]
            )
    product = None
    for g in range(3):
        whole = pair_ref[g]
        high = whole.astype(bf16)
        rest = whole - high.astype(f32)
        mid = rest.astype(bf16)
        low = (rest - mid.astype(f32)).astype(bf16)
        pieces = jnp.concatenate([high, mid, low], axis=0)
        factor = lax.dot_general(sel_ref[g], pieces, NN, preferred_element_type=f32)
        product = factor if product is None else product * factor
    basis = product * (1.0 / math.sqrt(POSES))
    basis_ref[...] = basis
    stack_ref[0:FIRST, :] = basis[0:FIRST]
    stack_ref[FIRST:STACK, :] = len_ref[...]

    sketch_ids = mus_rank * SKETCH_DEV + lax.broadcasted_iota(i32, (SKETCH_DEV, 1), 0)
    pose_ids = row_rank * POSE_DEV + lax.broadcasted_iota(i32, (1, POSE_DEV), 1)
    row_code = mod_m(3 * mix_round(mod_m(sketch_ids * 389 + seed)))
    pose_code = mod_m(mod_m(pose_ids) * 13 + seed)
    code = row_code + pose_code
    code = jnp.where(code >= modulus, code - modulus, code)
    hashed = mix_round(mix_round(code))
    sketch = ((hashed.astype(f32) + 0.5) * (2.0 / modulus) - 1.0) * math.sqrt(3.0 / SKETCH)
    both = dot3(split2(sketch), split2(stack_ref[...]), NT)
    for r in range(ROWS):
        z_ref[r, :, 0:STACK] = both[8 * r : 8 * r + 8]

    own_ref[...] = jnp.zeros_like(own_ref)
    for k in range(OWN):
        own_ref[k : k + 1, :] = len_ref[pl.ds(mus_rank * OWN + k, 1), :]
    right_ref[0:BLOCK, :] = basis_ref[pl.ds(pl.multiple_of(mus_rank * BLOCK, BLOCK), BLOCK), :]
    right_ref[BLOCK : 2 * BLOCK, :] = own_ref[...]
    columns = dot3(split2(basis), split2(right_ref[...]), NT)
    own = own_ref[...]
    squares = exact(jnp.ones((8, POSE_DEV), f32), own * own, NT)
    for r in range(ROWS):
        for k in range(4):
            at = BLOCK * r + 8 * k
            lane = STACK + BLOCK * k
            z_ref[r, :, lane : lane + BLOCK] = columns[at : at + 8, 0:BLOCK]
            z_ref[r, :, lane + 128 : lane + 128 + BLOCK] = columns[at : at + 8, BLOCK:]
    z_ref[ROWS - 1, :, STACK + 256 - BLOCK : STACK + 256] = squares


def gram_kernel(all_ref, out_ref):
    row_rank = lax.axis_index("rows")
    both = jnp.concatenate([all_ref[r, :, 0:STACK] for r in range(ROWS)], axis=0)
    turned = pltpu.roll(both[:, 0:PAD], lax.rem(PAD - row_rank * BLOCK, PAD), 1)
    block = dot3(split2(turned[:, 0:128]), split2(both), TN)
    out_ref[...] = jnp.zeros_like(out_ref)
    for m in range(MUS):
        for k in range(4):
            rows = block[8 * k : 8 * k + 8]
            lane = BLOCK * k
            muscle = FIRST + OWN * m
            out_ref[m, :, lane : lane + BLOCK] = rows[:, BLOCK * m : BLOCK * m + BLOCK]
            out_ref[m, :, lane + 128 : lane + 128 + OWN] = rows[:, muscle : muscle + OWN]


def place_kernel(tiles_ref, own_ref, out_ref, row_ref):
    for m in range(MUS):
        for k in range(4):
            at = BLOCK * m
            lane = BLOCK * k
            row_ref[8 * k : 8 * k + 8, at : at + BLOCK] = tiles_ref[m, :, lane : lane + BLOCK]
            row_ref[8 * k : 8 * k + 8, PAD + at : PAD + at + BLOCK] = tiles_ref[
                m, :, lane + 128 : lane + 128 + BLOCK
            ]
    half = BLOCK // 2
    core = lax.rem(lax.axis_index("mus"), 2)
    kept = row_ref[pl.ds(pl.multiple_of(core * half, half), half), :]
    own = own_ref[...]
    for r in range(ROWS):
        out_ref[r, :, 0 : 2 * PAD] = kept
        out_ref[r, 0:8, 2 * PAD :] = own
        out_ref[r, 8:half, 2 * PAD :] = jnp.zeros((half - 8, 256), f32)


def solve_kernel(
    mine_ref, theirs_ref, all_ref, basis_hbm, own_ref, coef_ref, res_ref,
    whole_ref, x_ref, mh_ref, ml_ref, xh_ref, xl_ref, gh_ref, gl_ref, c_ref, p_ref, basis_ref, sem,
):
    fetch = pltpu.make_async_copy(basis_hbm, basis_ref, sem)
    fetch.start()
    core = lax.rem(lax.axis_index("mus"), 2)
    half = BLOCK // 2

    def assemble(top_ref, bottom_ref):
        for r in range(ROWS):
            whole_ref[BLOCK * r : BLOCK * r + half, :] = top_ref[r, :, 0 : 2 * PAD]
            whole_ref[BLOCK * r + half : BLOCK * r + BLOCK, :] = bottom_ref[r, :, 0 : 2 * PAD]

    @pl.when(core == 0)
    def _():
        assemble(mine_ref, theirs_ref)

    @pl.when(core == 1)
    def _():
        assemble(theirs_ref, mine_ref)

    rows = lax.broadcasted_iota(i32, (PAD, PAD), 0)
    cols = lax.broadcasted_iota(i32, (PAD, PAD), 1)
    unit = (rows == cols).astype(f32)
    inside = (rows < TERMS) & (cols < TERMS)
    gram = jnp.where(inside, whole_ref[:, 0:PAD], unit)
    mh_ref[...], ml_ref[...] = split2(gram)
    gh_ref[...], gl_ref[...] = split2(jnp.where(inside, whole_ref[:, PAD : 2 * PAD], 0.0))
    c_ref[...] = jnp.zeros_like(c_ref)
    p_ref[...] = jnp.zeros_like(p_ref)
    for r in range(ROWS):
        for k in range(4):
            at = BLOCK * r + 8 * k
            lane = BLOCK * k
            c_ref[at : at + 8, 0:BLOCK] = all_ref[
                r, :, STACK + lane : STACK + lane + BLOCK
            ]
            p_ref[at : at + 8, 0:BLOCK] = mine_ref[
                r, 0:8, 2 * PAD + 128 + lane : 2 * PAD + 128 + lane + BLOCK
            ]
    c_all = c_ref[...]
    lengths2 = c_all[PAD - 1 : PAD, :]
    valid = lax.broadcasted_iota(i32, (PAD, 128), 0) < TERMS
    c_own = jnp.where(valid, c_all, 0.0)
    projected = jnp.where(valid, p_ref[...], 0.0)

    def plain(a, b):
        return lax.dot_general(a.astype(bf16), b.astype(bf16), NN, preferred_element_type=f32)

    frob = 1.0 / jnp.sqrt(jnp.sum(gram * gram))
    normed = (gram * frob).astype(bf16)
    square = plain(normed, normed)
    fourth = plain(square, square)
    bound = jnp.sqrt(jnp.sqrt(jnp.sqrt(jnp.sum(fourth * fourth))))
    scale = 1.84 * frob / bound
    x_ref[...] = (2.0 * scale) * unit - (scale * scale) * gram

    def coarse(_, carry):
        x = x_ref[...]
        high = x.astype(bf16)
        e = unit - plain(mh_ref[...], high)
        x_ref[...] = x + plain(high, e)
        return carry

    lax.fori_loop(0, 4, coarse, 0)

    def fine(state):
        step, _ = state
        x = x_ref[...]
        parts = split2(x)
        e = unit - dot3((mh_ref[...], ml_ref[...]), parts, NN)
        x_ref[...] = x + plain(parts[0], e)
        return step + 1, jnp.sum(e * e)

    lax.while_loop(lambda s: (s[0] < 40) & (s[1] > 1e-6), fine, (0, jnp.float32(1.0)))
    xh_ref[...], xl_ref[...] = split2(x_ref[...])

    left = lax.broadcasted_iota(i32, (PAD, 128), 1) < 64

    def times(high_ref, low_ref, b):
        high = b.astype(bf16).astype(f32)
        pieces = jnp.where(left, high, pltpu.roll(b - high, 64, 1)).astype(bf16)
        one = functools.partial(lax.dot_general, dimension_numbers=NN, preferred_element_type=f32)
        product = one(high_ref[...], pieces) + one(low_ref[...], pieces)
        return product + pltpu.roll(product, 64, 1)

    inv = functools.partial(times, xh_ref, xl_ref)
    apply_g = functools.partial(times, gh_ref, gl_ref)

    def total(a):
        return jnp.sum(a, axis=0, keepdims=True)

    start = inv(projected)
    g_start = apply_g(start)
    g_hat = c_own - g_start
    fresh2 = jnp.maximum(lengths2 - total(start * (c_own + g_hat)), 0.0)
    u_norm = jnp.sqrt(fresh2 + epsilon)
    g_hat = g_hat / u_norm
    u_square = fresh2 / (fresh2 + epsilon)
    t = inv(g_hat)
    v_norm = jnp.sqrt(jnp.maximum(total(g_hat * t), 0.0) + epsilon)
    v_hat = g_hat / v_norm
    t = t / v_norm
    w = t
    phi_bar = u_norm
    rot_bar = v_norm
    y = jnp.zeros_like(t)
    for step in range(ITERS):
        g_t = apply_g(t)
        fresh2 = jnp.maximum(
            total(t * (g_t - 2.0 * v_norm * g_hat)) + v_norm * v_norm * u_square, 0.0
        )
        u_norm = jnp.sqrt(fresh2 + epsilon)
        rot_norm = jnp.sqrt(rot_bar * rot_bar + u_norm * u_norm)
        cosine = rot_bar / rot_norm
        sine = u_norm / rot_norm
        y = y + (cosine * phi_bar / rot_norm) * w
        if step == ITERS - 1:
            break
        g_hat = (g_t - v_norm * g_hat) / u_norm
        u_square = fresh2 / (fresh2 + epsilon)
        q_hat = g_hat - u_norm * v_hat
        t = inv(q_hat)
        v_norm = jnp.sqrt(jnp.maximum(total(q_hat * t), 0.0) + epsilon)
        v_hat = q_hat / v_norm
        t = t / v_norm
        w = t - (sine * v_norm / rot_norm) * w
        rot_bar = -cosine * v_norm
        phi_bar = sine * phi_bar
    coef = jnp.transpose(start + y)
    coef_ref[...] = coef[0:OWN, 0:TERMS]
    fetch.wait()
    fitted = dot3(split2(coef[0:BLOCK]), split2(basis_ref[...]), NN)
    res_ref[...] = own_ref[0:OWN, :] - fitted[0:OWN]


def vmem():
    return pl.BlockSpec(memory_space=pltpu.VMEM)


def smem():
    return pl.BlockSpec(memory_space=pltpu.SMEM)


def per_device(sketch_seed, angles, lengths):
    selectors = jnp.asarray(pair_selectors(), dtype=bf16)

    z, basis, own = pl.pallas_call(
        local_kernel,
        out_shape=(
            jax.ShapeDtypeStruct((ROWS, 8, STACK + 256), f32),
            jax.ShapeDtypeStruct((PAD, POSE_DEV), f32),
            jax.ShapeDtypeStruct((BLOCK, POSE_DEV), f32),
        ),
        in_specs=[smem(), vmem(), vmem(), vmem()],
        out_specs=(vmem(), vmem(), vmem()),
        scratch_shapes=[
            pltpu.VMEM((3, PAIR, POSE_DEV), f32),
            pltpu.VMEM((STACK, POSE_DEV), f32),
            pltpu.VMEM((2 * BLOCK, POSE_DEV), f32),
        ],
        name="local_products",
    )(sketch_seed, angles, lengths, selectors)

    summed = jnp.sum(lax.all_to_all(z, "rows", 0, 0), axis=0)
    shared = jnp.concatenate([summed[:, 0:STACK], summed[:, STACK + 128 :]], axis=1)
    everyone = lax.all_to_all(
        jnp.broadcast_to(shared[None], (ROWS,) + shared.shape), "rows", 0, 0
    )

    parts = pl.pallas_call(
        gram_kernel,
        out_shape=jax.ShapeDtypeStruct((MUS, 8, 256), f32),
        in_specs=[vmem()],
        out_specs=vmem(),
        name="gram_block",
    )(everyone)
    tile = jnp.sum(lax.all_to_all(parts, "mus", 0, 0), axis=0)
    send = jnp.concatenate([tile[:, 0:128], summed[:, STACK : STACK + 128]], axis=1)
    tiles = lax.all_to_all(jnp.broadcast_to(send[None], (MUS,) + send.shape), "mus", 0, 0)

    half = BLOCK // 2
    kept = pl.pallas_call(
        place_kernel,
        out_shape=jax.ShapeDtypeStruct((ROWS, half, 2 * PAD + 256), f32),
        in_specs=[vmem(), vmem()],
        out_specs=vmem(),
        scratch_shapes=[pltpu.VMEM((BLOCK, 2 * PAD), f32)],
        name="place_rows",
    )(tiles, tile)
    mine = lax.all_to_all(kept, "rows", 0, 0)
    theirs = lax.ppermute(mine, "mus", [(i, i ^ 1) for i in range(MUS)])

    coef, residual = pl.pallas_call(
        solve_kernel,
        out_shape=(
            jax.ShapeDtypeStruct((OWN, TERMS), f32),
            jax.ShapeDtypeStruct((OWN, POSE_DEV), f32),
        ),
        in_specs=[vmem()] * 3 + [pl.BlockSpec(memory_space=pl.ANY), vmem()],
        out_specs=(vmem(), vmem()),
        scratch_shapes=[
            pltpu.VMEM((PAD, 2 * PAD), f32),
            pltpu.VMEM((PAD, PAD), f32),
        ]
        + [pltpu.VMEM((PAD, PAD), bf16)] * 6
        + [
            pltpu.VMEM((PAD, 128), f32),
            pltpu.VMEM((PAD, 128), f32),
            pltpu.VMEM((PAD, POSE_DEV), f32),
            pltpu.SemaphoreType.DMA(()),
        ],
        name="solve",
    )(mine, theirs, everyone, basis, own)
    return coef, residual


def solution(mesh):
    placed = (P(), P(None, "rows"), P(None, "rows"))
    return jax.shard_map(
        per_device,
        mesh=mesh,
        in_specs=placed,
        out_specs=(P("mus", None), P("mus", "rows")),
        check_vma=False,
    )
```
